32 devices in a mesh: groups: 2 (over x), pose: 16 (over z, y, core).
Axes of the slice: x: 2, y: 2, z: 4, core: 2. Of those that a mesh axis runs over, the one named last changes fastest.
Arguments:
- images: bfloat16 [32, 36864], P(('groups', 'pose')), parts along dimension 0
- ctf_class: int32 [32], P(('groups', 'pose')), parts along dimension 0, may hold values from 0 to 15
- projections: bfloat16 [2048, 36864], P(('groups', 'pose')), parts along dimension 0
- ctf_table: float32 [16, 18432], replicated, may hold values from 0.1 to 1
- tile_mask: int32 [2, 128], P('groups', 'pose'), parts along dimension 0, may hold values from 0 to 1, as said below
Outputs:
- back_sums: bfloat16 [2048, 36864], P(('groups', 'pose')), parts along dimension 0
- pose_totals: float32 [2048], P(('groups', 'pose')), parts along dimension 0
The draws below stay inside these ranges and needn't reach their ends.
There are 2 independent parts, one for each index of `groups`. The reference program is written for one: setup_inputs(seed, part) draws one part's arguments, and reference() takes and returns one part's arrays. A program takes and returns all parts, laid end to end along the dimension named above; an argument that names none is the same for every part. Nothing has to cross between parts.
Inputs may be any that keep to these rules, and one draw needn't show every extreme that they name: `tile_mask`: every block of 16 images has at least one significant tile of 8 poses.
All inputs are finite; a program needn't handle non-finite values.
Results may differ from the reference program's by a relative error of at most 0.0077.
Values may be sent and summed in bfloat16 or wider, within the bound.
No kernel may reach another device: no remote copies, remote signals or barrier semaphores. Data moves between devices by JAX's collectives and lax.ppermute only.
A program may use at most 128 MiB of HBM per device.

```python
import math
import jax
import jax.numpy as jnp
from jax import lax

BOX = 192
P_SIZE = 36864
NCTF = 16
NSHIFT = 5
IMG_TILE = 16
POSE_TILE = 8
NIMG = 16
NPOSE = 1024


def reference_row(key, pose_index):
    row_key = jax.random.fold_in(jax.random.fold_in(key, 2), pose_index)
    return jax.random.normal(row_key, (P_SIZE,), jnp.float32) * (3.0 / math.sqrt(P_SIZE))


def forced_tiles(key):
    return jax.random.randint(jax.random.fold_in(key, 7), (NIMG // IMG_TILE,), 0, NPOSE // POSE_TILE)


def draw_projections(key, part):
    pose_index = jnp.arange(NPOSE, dtype=jnp.int32)
    return jax.vmap(lambda index_value: reference_row(key, index_value))(pose_index).astype(jnp.bfloat16)


def draw_tile_mask(key, part):
    forced = forced_tiles(key)
    tile_count = NPOSE // POSE_TILE
    levels = jax.random.randint(jax.random.fold_in(key, 8), (tile_count,), 1, 7)
    rolls = jax.random.randint(jax.random.fold_in(key, 9), (NIMG // IMG_TILE, tile_count), 0, 8)
    columns = jnp.arange(tile_count, dtype=jnp.int32)
    chosen = (rolls < levels[None, :]) | (columns[None, :] == forced[:, None])
    return chosen.astype(jnp.int32)


def draw_images(key, part):
    noise = jax.random.normal(jax.random.fold_in(key, 1), (NIMG, P_SIZE), jnp.float32)
    return noise.astype(jnp.bfloat16)


def place_ends(entries, stream_key, least, top_value):
    index_at = [jax.random.randint(jax.random.fold_in(stream_key, axis), (), 0, length) for axis, length in enumerate(entries.shape)]
    longest = entries.shape.index(max(entries.shape))
    neighbour = index_at[:longest] + [(index_at[longest] + 1) % entries.shape[longest]] + index_at[longest + 1:]
    return entries.at[tuple(index_at)].set(least).at[tuple(neighbour)].set(top_value)


def setup_inputs(seed: int = 0, part: int = 0) -> dict:
    keys = jax.random.split(jax.random.key(seed), 6)
    part_splits = jax.random.split(jax.random.fold_in(keys[5], part), 6)
    images = draw_images(jax.random.fold_in(jax.random.fold_in(keys[5], part), 71), part)
    ctf_class = place_ends(jax.random.randint(part_splits[1], (NIMG,), 0, NCTF), jax.random.fold_in(part_splits[1], 1), 0, NCTF - 1).astype(jnp.int32)
    projections = draw_projections(jax.random.fold_in(jax.random.fold_in(keys[5], part), 71), part)
    ctf_table = jnp.clip(jax.random.uniform(keys[3], (NCTF, P_SIZE // 2), jnp.float32, 0.1, 1.0), 0.1, 1.0)
    tile_mask = draw_tile_mask(jax.random.fold_in(jax.random.fold_in(keys[5], part), 71), part)
    return dict(images=images, ctf_class=ctf_class, projections=projections, ctf_table=ctf_table, tile_mask=tile_mask)


shift_rows = (0.0, 1.0, -1.0, 0.0, 0.0)
shift_cols = (0.0, 0.0, 0.0, 1.0, -1.0)
floor_score = -1.0e30


def phase_tables(box_size):
    half_box = box_size // 2
    coeff_index = jnp.arange(box_size * half_box, dtype=jnp.int32)
    row_index = coeff_index // half_box
    col_index = coeff_index % half_box
    freq_x = jnp.where(row_index < half_box, row_index, row_index - box_size).astype(jnp.float32)
    freq_y = col_index.astype(jnp.float32)
    step_x = jnp.array(shift_rows, jnp.float32)[:, None]
    step_y = jnp.array(shift_cols, jnp.float32)[:, None]
    phases = (2.0 * math.pi / box_size) * (step_x * freq_x[None, :] + step_y * freq_y[None, :])
    return jnp.cos(phases), jnp.sin(phases)


def class_rows(classes, ctf_count):
    return (classes[:, None] == jnp.arange(ctf_count, dtype=jnp.int32)[None, :]).astype(jnp.float32)


def make_shifted(pixels, classes, ctf_table, cosine_tab, sine_table):
    half_len = pixels.shape[1] // 2
    one_hot = class_rows(classes, ctf_table.shape[0])
    factor = jnp.dot(one_hot, ctf_table, precision=lax.Precision.HIGHEST)[:, None, :]
    real_part = pixels[:, :half_len].astype(jnp.float32)[:, None, :]
    imag_part = pixels[:, half_len:].astype(jnp.float32)[:, None, :]
    shifted_re = (real_part * cosine_tab[None] + imag_part * sine_table[None]) * factor
    shifted_im = (imag_part * cosine_tab[None] - real_part * sine_table[None]) * factor
    return jnp.concatenate([shifted_re, shifted_im], axis=2).astype(jnp.bfloat16)


def norm_terms(projections, ctf_table):
    squared = ctf_table * ctf_table
    squared = jnp.concatenate([squared, squared], axis=1)
    proj_f = projections.astype(jnp.float32)
    return jnp.dot(squared, (proj_f * proj_f).T, precision=lax.Precision.HIGHEST)


def reference(images, ctf_class, projections, ctf_table, tile_mask):
    cosine_tab, sine_table = phase_tables(BOX)
    stacked = make_shifted(images, ctf_class, ctf_table, cosine_tab, sine_table).reshape(NIMG * NSHIFT, P_SIZE)
    norm_table = norm_terms(projections, ctf_table)
    penalty = jnp.dot(class_rows(ctf_class, NCTF), norm_table, precision=lax.Precision.HIGHEST)
    raw_scores = jnp.dot(stacked, projections.T, preferred_element_type=jnp.float32).reshape(NIMG, NSHIFT, NPOSE)
    scores = raw_scores - 0.5 * penalty[:, None, :]
    allowed = jnp.repeat(jnp.repeat(tile_mask, IMG_TILE, axis=0), POSE_TILE, axis=1) > 0
    masked = jnp.where(allowed[:, None, :], scores, floor_score)
    peak = jnp.max(masked, axis=(1, 2))
    exponent = jnp.where(allowed[:, None, :], jnp.exp(masked - peak[:, None, None]), 0.0)
    denominator = jnp.sum(exponent, axis=(1, 2))
    weights = (exponent / denominator[:, None, None]).astype(jnp.bfloat16)
    rescale = NSHIFT * NPOSE / NIMG
    accumulated = lax.dot_general(weights.reshape(NIMG * NSHIFT, NPOSE), stacked, (((0,), (0,)), ((), ())), preferred_element_type=jnp.float32)
    back_sums = (rescale * accumulated).astype(jnp.bfloat16)
    pose_totals = rescale * jnp.sum(weights.astype(jnp.float32), axis=(0, 1))
    return back_sums, pose_totals
```

```python
import functools
import math

import jax
import jax.numpy as jnp
import numpy as np
from jax import lax
from jax.experimental import pallas as pl
from jax.experimental.pallas import tpu as pltpu
from jax.sharding import PartitionSpec as P

BOX = 192
IMG_TILE = 16
POSE_TILE = 8
LANES = 128
GROUP = 8
SHIFTS = 5
FLOOR = -1e30
F32 = jnp.float32
BF16 = jnp.bfloat16


def phase_tables():
    half = BOX // 2
    index = np.arange(BOX * half)
    row, col = index // half, index % half
    freq_x = np.where(row < half, row, row - BOX).astype(np.float64)
    freq_y = col.astype(np.float64)
    step = 2.0 * math.pi / BOX
    tables = [np.cos(step * freq_x), np.sin(step * freq_x), np.cos(step * freq_y), np.sin(step * freq_y)]
    return np.stack(tables).astype(np.float32).reshape(4, -1, LANES)


def pick_rows(table, rows):
    picked = jnp.zeros(rows.shape, table.dtype)
    for base in range(0, table.shape[0], 8):
        part = jnp.take_along_axis(table[base : base + 8], rows & 7, axis=0)
        picked = jnp.where((rows >> 3) == base // 8, part, picked)
    return picked


def norm_kernel(proj_re, proj_im, ctf, out):
    @pl.when(pl.program_id(0) == 0)
    def _():
        out[...] = jnp.zeros_like(out)

    real, imag = proj_re[...].astype(F32), proj_im[...].astype(F32)
    power = real * real + imag * imag
    power_hi = power.astype(BF16)
    power_lo = (power - power_hi.astype(F32)).astype(BF16)
    gain = ctf[...] * ctf[...]
    gain_hi = gain.astype(BF16)
    gain_lo = (gain - gain_hi.astype(F32)).astype(BF16)
    dims = (((1,), (1,)), ((), ()))
    dot = functools.partial(lax.dot_general, dimension_numbers=dims, preferred_element_type=F32)
    out[...] += dot(gain_hi, power_hi) + (dot(gain_hi, power_lo) + dot(gain_lo, power_hi))


def norm_table(projections, ctf_table, chunk):
    poses, width = projections.shape
    half = width // 2
    classes = ctf_table.shape[0]
    steps = half // chunk
    return pl.pallas_call(
        norm_kernel,
        grid=(steps,),
        in_specs=[
            pl.BlockSpec((poses, chunk), lambda j: (0, j)),
            pl.BlockSpec((poses, chunk), lambda j: (0, j + steps)),
            pl.BlockSpec((classes, chunk), lambda j: (0, j)),
        ],
        out_specs=pl.BlockSpec((classes, poses), lambda j: (0, 0)),
        out_shape=jax.ShapeDtypeStruct((classes, poses), F32),
        compiler_params=pltpu.CompilerParams(vmem_limit_bytes=24 << 20),
        cost_estimate=pl.CostEstimate(flops=8 << 20, bytes_accessed=projections.size * 2, transcendentals=0),
        name="norm",
    )(projections, projections, ctf_table)


def score_kernel(chunk, stride, img, ctf, tab, proj_re, proj_im, shifted, raw, wide):
    step = pl.program_id(0)

    @pl.when(step == 0)
    def _():
        wide[...] = img[...].astype(F32)
        raw[...] = jnp.zeros_like(raw)

    half_rows = tab.shape[1]
    tiles = chunk // LANES
    classes = wide[pl.ds(2 * half_rows, GROUP, stride=stride), :].astype(jnp.int32)
    for tile in range(tiles):
        row = step * tiles + tile
        lanes = pl.ds(tile * LANES, LANES)
        gain = pick_rows(ctf[:, lanes], classes)
        real = wide[pl.ds(row, GROUP, stride=stride), :] * gain
        imag = wide[pl.ds(row + half_rows, GROUP, stride=stride), :] * gain
        trig = [jnp.broadcast_to(tab[axis, pl.ds(row, 1), :], (GROUP, LANES)) for axis in range(4)]
        out_re, out_im = [real], [imag]
        for cos, sin in (trig[:2], trig[2:]):
            rc, si, ic, sr = real * cos, imag * sin, imag * cos, real * sin
            out_re += [rc + si, rc - si]
            out_im += [ic - sr, ic + sr]
        shifted[0, :, lanes] = jnp.concatenate(out_re, axis=0).astype(BF16)
        shifted[1, :, lanes] = jnp.concatenate(out_im, axis=0).astype(BF16)
    dims = (((1,), (1,)), ((), ()))
    raw[...] += lax.dot_general(shifted[0], proj_re[...], dims, preferred_element_type=F32)
    raw[...] += lax.dot_general(shifted[1], proj_im[...], dims, preferred_element_type=F32)


def score_group(pixels, ctf_table, tables, projections, chunk):
    poses, width = projections.shape
    half = width // 2
    steps = half // chunk
    rows = SHIFTS * GROUP
    stride = pixels.shape[1]
    return pl.pallas_call(
        functools.partial(score_kernel, chunk, stride),
        grid=(steps,),
        in_specs=[
            pl.BlockSpec((GROUP * stride, LANES), lambda j: (0, 0)),
            pl.BlockSpec((ctf_table.shape[0], chunk), lambda j: (0, j)),
            pl.BlockSpec(tables.shape, lambda j: (0, 0, 0)),
            pl.BlockSpec((poses, chunk), lambda j: (0, j)),
            pl.BlockSpec((poses, chunk), lambda j: (0, j + steps)),
        ],
        out_specs=[
            pl.BlockSpec((2, rows, chunk), lambda j: (0, 0, j)),
            pl.BlockSpec((rows, poses), lambda j: (0, 0)),
        ],
        out_shape=[
            jax.ShapeDtypeStruct((2, rows, half), BF16),
            jax.ShapeDtypeStruct((rows, poses), F32),
        ],
        scratch_shapes=[pltpu.VMEM((GROUP * stride, LANES), F32)],
        compiler_params=pltpu.CompilerParams(vmem_limit_bytes=24 << 20),
        cost_estimate=pl.CostEstimate(flops=64 << 20, bytes_accessed=projections.size * 2, transcendentals=0),
        name="score",
    )(pixels.reshape(GROUP * stride, LANES), ctf_table, tables, projections, projections)


def owner_column(place, me):
    return place ^ me


def allowed_poses(mask, owner, poses):
    pose = lax.broadcasted_iota(jnp.int32, (GROUP, poses), 1) // POSE_TILE
    tile = owner[:, :poses] // IMG_TILE
    picked = jnp.zeros((GROUP, poses), jnp.int32)
    for i in range(mask.shape[0]):
        for k in range(mask.shape[1]):
            picked = jnp.where((pose == k) & (tile == i), mask[i, k], picked)
    return picked > 0


def masked_scores(raw, norm, classes, allowed):
    poses = raw.shape[1]
    penalty = 0.5 * pick_rows(norm[...], classes[:, :poses])
    scores = raw[...].reshape(SHIFTS, GROUP, poses) - penalty[None]
    return jnp.where(allowed[None], scores, FLOOR)


def stats_kernel(groups, *refs):
    raws, cls = refs[:groups], refs[groups : 2 * groups]
    norm, place, mask, out, masked_out = refs[2 * groups :]
    me = lax.axis_index("pose")
    lane = lax.broadcasted_iota(jnp.int32, (GROUP, LANES), 1)
    poses = norm.shape[1]
    peaks = jnp.zeros((1, LANES), F32)
    totals = jnp.zeros((1, LANES), F32)
    for g in range(groups):
        owner = owner_column(place[g], me)
        allowed = allowed_poses(mask, owner, poses)
        masked = masked_scores(raws[g], norm, cls[g][...].astype(jnp.int32), allowed)
        masked_out[g] = masked.reshape(SHIFTS * GROUP, poses)
        peak = jnp.max(jnp.max(masked, axis=0), axis=1, keepdims=True)
        exps = jnp.where(allowed[None], jnp.exp(masked - peak[None]), 0.0)
        total = jnp.sum(jnp.sum(exps, axis=0), axis=1, keepdims=True)
        mine = lane == owner
        peaks += jnp.sum(jnp.where(mine, peak, 0.0), axis=0, keepdims=True)
        totals += jnp.sum(jnp.where(mine, total, 0.0), axis=0, keepdims=True)
    out[...] = jnp.concatenate([peaks, totals], axis=0)


def local_stats(raws, classes, norm, place, mask):
    groups = len(raws)
    poses = norm.shape[1]
    vmem = pl.BlockSpec(memory_space=pltpu.VMEM)
    return pl.pallas_call(
        functools.partial(stats_kernel, groups),
        in_specs=[vmem] * (2 * groups + 2) + [pl.BlockSpec(memory_space=pltpu.SMEM)],
        out_specs=[vmem, vmem],
        out_shape=[
            jax.ShapeDtypeStruct((2, LANES), F32),
            jax.ShapeDtypeStruct((groups, SHIFTS * GROUP, poses), F32),
        ],
        compiler_params=pltpu.CompilerParams(vmem_limit_bytes=24 << 20),
        name="stats",
    )(*raws, *classes, norm, place, mask)


def sums_kernel(groups, rescale, stats, masked, place, *refs):
    shifted, (out, pose_totals, weight) = refs[:groups], refs[groups:]

    @pl.when((pl.program_id(0) == 0) & (pl.program_id(1) == 0))
    def _():
        me = lax.axis_index("pose")
        lane = lax.broadcasted_iota(jnp.int32, (GROUP, LANES), 1)
        peaks, totals = stats[:, 0, :], stats[:, 1, :]
        top = jnp.max(peaks, axis=0, keepdims=True)
        bottom = jnp.sum(totals * jnp.exp(peaks - top), axis=0, keepdims=True)
        pose_sum = jnp.zeros(pose_totals.shape, F32)
        for g in range(groups):
            mine = lane == owner_column(place[g], me)
            peak = jnp.sum(jnp.where(mine, top, 0.0), axis=1, keepdims=True)
            total = jnp.sum(jnp.where(mine, bottom, 0.0), axis=1, keepdims=True)
            scores = masked[g].reshape(SHIFTS, GROUP, -1)
            exps = jnp.where(scores > 0.5 * FLOOR, jnp.exp(scores - peak[None]), 0.0)
            rounded = (exps / total[None]).astype(BF16).astype(F32).reshape(SHIFTS * GROUP, -1)
            weight[g] = rounded.T.astype(BF16)
            pose_sum += jnp.sum(rounded, axis=0, keepdims=True)
        pose_totals[...] = rescale * pose_sum

    dims = (((1,), (0,)), ((), ()))
    total = lax.dot_general(weight[0], shifted[0][0], dims, preferred_element_type=F32)
    for g in range(1, groups):
        total += lax.dot_general(weight[g], shifted[g][0], dims, preferred_element_type=F32)
    out[...] = (rescale * total).astype(BF16)


def weighted_sums(stats, masked, place, shifted, rescale, chunk):
    groups, rows, poses = masked.shape
    half = shifted[0].shape[2]
    steps = half // chunk
    full = lambda shape: pl.BlockSpec(shape, lambda h, j: (0,) * len(shape))
    return pl.pallas_call(
        functools.partial(sums_kernel, groups, rescale),
        grid=(2, steps),
        in_specs=[full(stats.shape), full(masked.shape), full(place.shape)]
        + [pl.BlockSpec((1, rows, chunk), lambda h, j: (h, 0, j))] * groups,
        out_specs=[
            pl.BlockSpec((poses, chunk), lambda h, j: (0, h * steps + j)),
            full((1, poses)),
        ],
        out_shape=[
            jax.ShapeDtypeStruct((poses, 2 * half), BF16),
            jax.ShapeDtypeStruct((1, poses), F32),
        ],
        scratch_shapes=[pltpu.VMEM((groups, poses, rows), BF16)],
        compiler_params=pltpu.CompilerParams(vmem_limit_bytes=24 << 20),
        name="sums",
    )(stats, masked, place, *shifted)


def gathered(message, axis, size):
    offsets, stacked = [0], message[None]
    bit = size // 2
    while bit:
        pairs = [(i, i ^ bit) for i in range(size)]
        stacked = jnp.concatenate([stacked, lax.ppermute(stacked, axis, pairs)])
        offsets += [o ^ bit for o in offsets]
        bit //= 2
    return stacked, offsets


def per_device(size, images, ctf_class, projections, ctf_table, tile_mask):
    poses, width = projections.shape
    per_chunk = 2048
    rows = width // LANES
    rescale = SHIFTS * poses / images.shape[0]
    tables = jnp.asarray(phase_tables())
    cls_rows = jnp.broadcast_to(ctf_class.astype(BF16)[:, None], (8, LANES))
    message = jnp.concatenate([images.reshape(rows, LANES), cls_rows])
    norm = norm_table(projections, ctf_table, per_chunk)
    stacked, offsets = gathered(message, "pose", size)
    groups = size // GROUP
    place = jnp.asarray(np.broadcast_to(np.array(offsets, np.int32).reshape(groups, GROUP, 1), (groups, GROUP, LANES)))
    raws, shifted, classes = [], [], []
    for g in range(groups):
        pixels = stacked[g * GROUP : (g + 1) * GROUP]
        moved, raw = score_group(pixels, ctf_table, tables, projections, per_chunk)
        shifted.append(moved)
        raws.append(raw)
        classes.append(pixels[:, rows, :].astype(F32))
    stats, masked = local_stats(raws, classes, norm, place, tile_mask)
    everyone = lax.all_to_all(jnp.broadcast_to(stats[None], (size, 2, LANES)), "pose", 0, 0)
    back_sums, pose_totals = weighted_sums(everyone, masked, place, shifted, rescale, per_chunk)
    return back_sums, pose_totals[0]


def solution(mesh):
    in_specs = (
        P(("groups", "pose"), None),
        P(("groups", "pose")),
        P(("groups", "pose"), None),
        P(),
        P("groups", "pose"),
    )
    out_specs = (P(("groups", "pose"), None), P(("groups", "pose")))
    return jax.shard_map(
        functools.partial(per_device, mesh.shape["pose"]),
        mesh=mesh,
        in_specs=in_specs,
        out_specs=out_specs,
        check_vma=False,
    )
```

```python
import functools
import math

import jax
import jax.numpy as jnp
import numpy as np
from jax import lax
from jax.experimental import pallas as pl
from jax.experimental.pallas import tpu as pltpu
from jax.sharding import PartitionSpec as P


BOX = 192
IMG_TILE = 16
POSE_TILE = 8
LANES = 128
GROUP = 8
SHIFTS = 5
FLOOR = -1e30
F32 = jnp.float32
BF16 = jnp.bfloat16


def phase_tables():
    half = BOX // 2
    index = np.arange(BOX * half)
    row, col = index // half, index % half
    freq_x = np.where(row < half, row, row - BOX).astype(np.float64)
    freq_y = col.astype(np.float64)
    step = 2.0 * math.pi / BOX
    tables = [np.cos(step * freq_x), np.sin(step * freq_x), np.cos(step * freq_y), np.sin(step * freq_y)]
    return np.stack(tables).astype(np.float32).reshape(4, -1, LANES)


def pick_rows(table, rows):
    picked = jnp.zeros(rows.shape, table.dtype)
    for base in range(0, table.shape[0], 8):
        part = jnp.take_along_axis(table[base : base + 8], rows & 7, axis=0)
        picked = jnp.where((rows >> 3) == base // 8, part, picked)
    return picked


def norm_kernel(pieces, block, proj, ctf, held, out, arrive):
    _, width = held.shape
    half = width // 2
    span = half // pieces

    def fetch(index, part):
        lanes = pl.ds(part * half + index * span, span)
        return pltpu.make_async_copy(proj.at[:, lanes], held.at[:, lanes], arrive.at[part, index])

    for index in range(pieces):
        for part in range(2):
            fetch(index, part).start()
    dims = (((1,), (1,)), ((), ()))
    dot = functools.partial(lax.dot_general, dimension_numbers=dims, preferred_element_type=F32)

    def add(index, total):
        at = index * block
        real = held[:, pl.ds(at, block)].astype(F32)
        imag = held[:, pl.ds(half + at, block)].astype(F32)
        power = real * real + imag * imag
        power_hi = power.astype(BF16)
        power_lo = (power - power_hi.astype(F32)).astype(BF16)
        gain = ctf[:, pl.ds(at, block)]
        gain = gain * gain
        gain_hi = gain.astype(BF16)
        gain_lo = (gain - gain_hi.astype(F32)).astype(BF16)
        both = dot(jnp.concatenate([gain_hi, gain_lo], axis=0), power_hi)
        count = gain.shape[0]
        return total + ((both[:count] + both[count:]) + dot(gain_hi, power_lo))

    total = jnp.zeros(out.shape, F32)
    for index in range(pieces):
        for part in range(2):
            fetch(index, part).wait()
        low = index * span // block
        for at in range(low, low + span // block):
            total = add(at, total)
    out[...] = total


def norm_table(projections, ctf_table):
    poses, width = projections.shape
    classes = ctf_table.shape[0]
    pieces = 9
    return pl.pallas_call(
        functools.partial(norm_kernel, pieces, 512),
        in_specs=[pl.BlockSpec(memory_space=pltpu.HBM), pl.BlockSpec(memory_space=pltpu.VMEM)],
        out_specs=[pl.BlockSpec(memory_space=pltpu.VMEM)] * 2,
        out_shape=[pltpu.VMEM((poses, width), BF16), pltpu.VMEM((classes, poses), F32)],
        scratch_shapes=[pltpu.SemaphoreType.DMA((2, pieces))],
        compiler_params=pltpu.CompilerParams(vmem_limit_bytes=8 << 20),
        cost_estimate=pl.CostEstimate(flops=1 << 30, bytes_accessed=projections.size * 2, transcendentals=0),
        name="norm",
    )(projections, ctf_table)


def score_kernel(stride, counts, ctf, tab, proj, *refs):
    imgs, (shifted, raw, cls, wide) = refs[: len(counts)], refs[len(counts) :]
    half_rows = tab.shape[1]
    base = 0
    for img, count in zip(imgs, counts):
        wide[pl.ds(base * stride, count * stride), :] = img[...].astype(F32)
        base += count
    classes = wide[pl.ds(2 * half_rows, GROUP, stride=stride), :].astype(jnp.int32)
    cls[...] = classes
    half = half_rows * LANES
    tiles = 8
    chunk = tiles * LANES
    dims = (((1,), (1,)), ((), ()))
    dot = functools.partial(lax.dot_general, dimension_numbers=dims, preferred_element_type=F32)

    def add(step, total):
        at = step * chunk
        for tile in range(tiles):
            row = step * tiles + tile
            lanes = pl.ds(at + tile * LANES, LANES)
            lanes_im = pl.ds(half + at + tile * LANES, LANES)
            gain = pick_rows(ctf[:, lanes], classes)
            real = wide[pl.ds(row, GROUP, stride=stride), :] * gain
            imag = wide[pl.ds(row + half_rows, GROUP, stride=stride), :] * gain
            trig = [jnp.broadcast_to(tab[axis, pl.ds(row, 1), :], (GROUP, LANES)) for axis in range(4)]
            out_re, out_im = [real], [imag]
            for cos, sin in (trig[:2], trig[2:]):
                rc, si, ic, sr = real * cos, imag * sin, imag * cos, real * sin
                out_re += [rc + si, rc - si]
                out_im += [ic - sr, ic + sr]
            shifted[:, lanes] = jnp.concatenate(out_re, axis=0).astype(BF16)
            shifted[:, lanes_im] = jnp.concatenate(out_im, axis=0).astype(BF16)
        re, im = pl.ds(at, chunk), pl.ds(half + at, chunk)
        return total + (dot(shifted[:, re], proj[:, re]) + dot(shifted[:, im], proj[:, im]))

    total = jnp.zeros(raw.shape, F32)
    for step in range(half // chunk):
        total = add(step, total)
    raw[...] = total


def score_group(pixels, ctf_table, tables, held, small):
    poses, width = held.shape
    rows = SHIFTS * GROUP
    stride = width // LANES + 8
    counts = [p.shape[0] // stride for p in pixels]
    vmem = pl.BlockSpec(memory_space=pltpu.VMEM)
    return pl.pallas_call(
        functools.partial(score_kernel, stride, counts),
        in_specs=[vmem] * (3 + len(pixels)),
        out_specs=[vmem] * 3,
        out_shape=[
            (pltpu.VMEM if small else jax.ShapeDtypeStruct)((rows, width), BF16),
            pltpu.VMEM((rows, poses), F32),
            pltpu.VMEM((GROUP, LANES), jnp.int32),
        ],
        scratch_shapes=[pltpu.VMEM((GROUP * stride, LANES), F32)],
        compiler_params=pltpu.CompilerParams(vmem_limit_bytes=(8 if small else 16) << 20),
        cost_estimate=pl.CostEstimate(flops=1 << 30, bytes_accessed=4 << 20, transcendentals=0),
        name="score",
    )(ctf_table, tables, held, *pixels)


def owner_column(place, me):
    return place ^ me


def allowed_poses(mask, owner, poses):
    pose = lax.broadcasted_iota(jnp.int32, (GROUP, poses), 1) // POSE_TILE
    tile = owner[:, :poses] // IMG_TILE
    picked = jnp.zeros((GROUP, poses), jnp.int32)
    for i in range(mask.shape[0]):
        for k in range(mask.shape[1]):
            picked = jnp.where((pose == k) & (tile == i), mask[i, k], picked)
    return picked > 0


def masked_scores(raw, norm, classes, allowed):
    poses = raw.shape[1]
    penalty = 0.5 * pick_rows(norm[...], classes[:, :poses])
    scores = raw[...].reshape(SHIFTS, GROUP, poses) - penalty[None]
    return jnp.where(allowed[None], scores, FLOOR)


def stats_kernel(groups, *refs):
    raws, cls = refs[:groups], refs[groups : 2 * groups]
    norm, place, mask, out, masked_out = refs[2 * groups :]
    me = lax.axis_index("pose")
    lane = lax.broadcasted_iota(jnp.int32, (GROUP, LANES), 1)
    poses = norm.shape[1]
    peaks = jnp.zeros((1, LANES), F32)
    totals = jnp.zeros((1, LANES), F32)
    for g in range(groups):
        owner = owner_column(place[g], me)
        allowed = allowed_poses(mask, owner, poses)
        masked = masked_scores(raws[g], norm, cls[g][...], allowed)
        masked_out[g] = masked.reshape(SHIFTS * GROUP, poses)
        peak = jnp.max(jnp.max(masked, axis=0), axis=1, keepdims=True)
        exps = jnp.where(allowed[None], jnp.exp(masked - peak[None]), 0.0)
        total = jnp.sum(jnp.sum(exps, axis=0), axis=1, keepdims=True)
        mine = lane == owner
        peaks += jnp.sum(jnp.where(mine, peak, 0.0), axis=0, keepdims=True)
        totals += jnp.sum(jnp.where(mine, total, 0.0), axis=0, keepdims=True)
    out[...] = jnp.concatenate([peaks, totals], axis=0)


def local_stats(raws, classes, norm, place, mask):
    groups = len(raws)
    poses = norm.shape[1]
    vmem = pl.BlockSpec(memory_space=pltpu.VMEM)
    return pl.pallas_call(
        functools.partial(stats_kernel, groups),
        in_specs=[vmem] * (2 * groups + 2) + [pl.BlockSpec(memory_space=pltpu.SMEM)],
        out_specs=[vmem, vmem],
        out_shape=[
            jax.ShapeDtypeStruct((2, LANES), F32),
            jax.ShapeDtypeStruct((groups, SHIFTS * GROUP, poses), F32),
        ],
        compiler_params=pltpu.CompilerParams(vmem_limit_bytes=24 << 20),
        name="stats",
    )(*raws, *classes, norm, place, mask)


def fill_weights(rescale, stats, masked, place, pose_totals, weight):
    me = lax.axis_index("pose")
    lane = lax.broadcasted_iota(jnp.int32, (GROUP, LANES), 1)
    peaks, totals = stats[:, 0, :], stats[:, 1, :]
    top = jnp.max(peaks, axis=0, keepdims=True)
    bottom = jnp.sum(totals * jnp.exp(peaks - top), axis=0, keepdims=True)
    pose_sum = jnp.zeros(pose_totals.shape, F32)
    for g in range(masked.shape[0]):
        mine = lane == owner_column(place[g], me)
        peak = jnp.sum(jnp.where(mine, top, 0.0), axis=1, keepdims=True)
        total = jnp.sum(jnp.where(mine, bottom, 0.0), axis=1, keepdims=True)
        scores = masked[g].reshape(SHIFTS, GROUP, -1)
        exps = jnp.where(scores > 0.5 * FLOOR, jnp.exp(scores - peak[None]), 0.0)
        rounded = (exps / total[None]).astype(BF16).astype(F32).reshape(SHIFTS * GROUP, -1)
        weight[g] = rounded.T.astype(BF16)
        pose_sum += jnp.sum(rounded, axis=0, keepdims=True)
    pose_totals[...] = rescale * pose_sum


def sums_kernel(groups, rescale, stats, masked, place, *refs):
    shifted, (out, pose_totals, weight, held, leave) = refs[:groups], refs[groups:]
    fill_weights(rescale, stats, masked, place, pose_totals, weight)
    width = out.shape[1]
    pieces, block = leave.shape[0], 512
    span = width // pieces
    dims = (((1,), (0,)), ((), ()))

    def fill(index):
        lanes = pl.ds(index * block, block)
        total = lax.dot_general(weight[0], shifted[0][:, lanes], dims, preferred_element_type=F32)
        for g in range(1, groups):
            total += lax.dot_general(weight[g], shifted[g][:, lanes], dims, preferred_element_type=F32)
        held[:, lanes] = (rescale * total).astype(BF16)

    def send(piece):
        lanes = pl.ds(piece * span, span)
        return pltpu.make_async_copy(held.at[:, lanes], out.at[:, lanes], leave.at[piece])

    for piece in range(pieces):
        low = piece * span // block
        for index in range(low, low + span // block):
            fill(index)
        send(piece).start()
    for piece in range(pieces):
        send(piece).wait()


def weighted_sums(stats, masked, place, shifted, rescale):
    groups, rows, poses = masked.shape
    width = shifted[0].shape[1]
    vmem = pl.BlockSpec(memory_space=pltpu.VMEM)
    return pl.pallas_call(
        functools.partial(sums_kernel, groups, rescale),
        in_specs=[vmem] * (3 + groups),
        out_specs=[pl.BlockSpec(memory_space=pl.ANY), vmem],
        out_shape=[
            jax.ShapeDtypeStruct((poses, width), BF16),
            jax.ShapeDtypeStruct((1, poses), F32),
        ],
        scratch_shapes=[
            pltpu.VMEM((groups, poses, rows), BF16),
            pltpu.VMEM((poses, width), BF16),
            pltpu.SemaphoreType.DMA((9,)),
        ],
        compiler_params=pltpu.CompilerParams(vmem_limit_bytes=8 << 20),
        name="sums",
    )(stats, masked, place, *shifted)


def streamed_kernel(groups, rescale, stats, masked, place, *refs):
    shifted, (out, pose_totals, weight) = refs[:groups], refs[groups:]

    @pl.when(pl.program_id(0) == 0)
    def _():
        fill_weights(rescale, stats, masked, place, pose_totals, weight)

    dims = (((1,), (0,)), ((), ()))
    total = jnp.zeros(out.shape, F32)
    for g in range(groups):
        total += lax.dot_general(weight[g], shifted[g][...], dims, preferred_element_type=F32)
    out[...] = (rescale * total).astype(BF16)


def streamed_sums(stats, masked, place, shifted, rescale):
    groups, rows, poses = masked.shape
    width = shifted[0].shape[1]
    chunk = 2048
    full = lambda shape: pl.BlockSpec(shape, lambda j: (0,) * len(shape))
    return pl.pallas_call(
        functools.partial(streamed_kernel, groups, rescale),
        grid=(width // chunk,),
        in_specs=[full(stats.shape), full(masked.shape), full(place.shape)]
        + [pl.BlockSpec((rows, chunk), lambda j: (0, j))] * groups,
        out_specs=[pl.BlockSpec((poses, chunk), lambda j: (0, j)), full((1, poses))],
        out_shape=[
            jax.ShapeDtypeStruct((poses, width), BF16),
            jax.ShapeDtypeStruct((1, poses), F32),
        ],
        scratch_shapes=[pltpu.VMEM((groups, poses, rows), BF16)],
        compiler_params=pltpu.CompilerParams(vmem_limit_bytes=24 << 20),
        name="streamed",
    )(stats, masked, place, *shifted)


def split_groups(parts, stride):
    pieces, offsets = [], []
    for value, owners in parts:
        for low in range(0, len(owners), GROUP):
            some = owners[low : low + GROUP]
            pieces.append(value[low * stride : (low + len(some)) * stride] if len(some) < len(owners) else value)
            offsets += some
            if len(offsets) == GROUP:
                yield pieces, offsets
                pieces, offsets = [], []
    assert not offsets


def per_device(size, images, ctf_class, projections, ctf_table, tile_mask):
    poses, width = projections.shape
    rows = width // LANES
    rescale = SHIFTS * poses / images.shape[0]
    tables = jnp.asarray(phase_tables())
    cls_rows = jnp.broadcast_to(ctf_class.astype(BF16)[:, None], (8, LANES))
    message = jnp.concatenate([images.reshape(rows, LANES), cls_rows])

    def swap(held, bit):
        value, offsets = held
        moved = lax.ppermute(value, "pose", [(i, i ^ bit) for i in range(size)])
        return moved, [o ^ bit for o in offsets]

    def joined(left, right):
        return jnp.concatenate([left[0], right[0]]), left[1] + right[1]

    held, norm = norm_table(pltpu.with_memory_space_constraint(projections, pltpu.HBM), ctf_table)
    unit = (message, [0])
    bit = size // 2
    while bit > 8:
        unit = joined(unit, swap(unit, bit))
        bit //= 2
    pair = joined(unit, swap(unit, 8))
    z1 = swap(pair, 4)
    y1 = swap(pair, 2)
    c1 = swap(pair, 1)
    y2 = swap(z1, 2)
    c2 = swap(z1, 1)
    c3 = swap(y1, 1)
    c4 = swap(y2, 1)
    groups = size // GROUP
    small = groups * SHIFTS * GROUP * width * 2 <= 8 << 20
    raws, shifted, classes, places = [], [], [], []
    for parts in ([pair, z1, c1, c2], [y1, y2, c3, c4]):
        for pixels, offsets in split_groups(parts, rows + 8):
            moved, raw, cls = score_group(pixels, ctf_table, tables, held, small)
            shifted.append(moved)
            raws.append(raw)
            classes.append(cls)
            places.append(offsets)
    place = jnp.asarray(np.broadcast_to(np.array(places, np.int32)[:, :, None], (groups, GROUP, LANES)))
    stats, masked = local_stats(raws, classes, norm, place, tile_mask)
    everyone = lax.all_to_all(jnp.broadcast_to(stats[None], (size, 2, LANES)), "pose", 0, 0)
    sums = weighted_sums if small else streamed_sums
    back_sums, pose_totals = sums(everyone, masked, place, shifted, rescale)
    return back_sums, pose_totals[0]


def solution(mesh):
    in_specs = (
        P(("groups", "pose"), None),
        P(("groups", "pose")),
        P(("groups", "pose"), None),
        P(),
        P("groups", "pose"),
    )
    out_specs = (P(("groups", "pose"), None), P(("groups", "pose")))

    def body(*args):
        return per_device(mesh.shape["pose"], *args)

    return jax.shard_map(
        body,
        mesh=mesh,
        in_specs=in_specs,
        out_specs=out_specs,
        check_vma=False,
    )
```
